32 devices in a mesh: chan: 4 (over x, core), seq: 8 (over z, y).
Axes of the slice: x: 2, y: 2, z: 4, core: 2. Of those that a mesh axis runs over, the one named last changes fastest.
Arguments:
- query: bfloat16 [4096, 512], P('seq', 'chan'), may hold values from -6 to 6
- key: bfloat16 [4096, 512], P('seq', 'chan'), may hold values from -6 to 6
- value: bfloat16 [4096, 512], P('seq', 'chan'), may hold values from -6 to 6
- filter_weights: bfloat16 [512, 8, 512], P('chan', 'seq'), may hold values from -6 to 6
- skip_gain: float32 [512], P('chan'), may hold values from 0.5 to 1.5
- cotangent: bfloat16 [4096, 512], P('seq', 'chan'), may hold values from -6 to 6
Outputs:
- mixed: bfloat16 [4096, 512], P('seq', 'chan')
- query_grad: bfloat16 [4096, 512], P('seq', 'chan')
- key_grad: bfloat16 [4096, 512], P('seq', 'chan')
- value_grad: bfloat16 [4096, 512], P('seq', 'chan')
- filter_grad: float32 [512, 8, 512], P('chan', 'seq')
The draws below stay inside these ranges and needn't reach their ends.
All inputs are finite; a program needn't handle non-finite values.
Results may differ from the reference program's by a relative error of at most 0.0085.
Values may be sent and summed in bfloat16 or wider, within the bound.
A program may use at most 64 MiB of HBM per device.

```python
import math
import jax
import jax.numpy as jnp
from jax import lax

TOK_DEV = 512
CH_DEV = 128
TOKENS = 4096
CHANNELS = 512
N_CHAN = 4
N_SEQ = 8


def levels(key, dims, split, low, top_value):
    level, own = 1.0, jax.random.fold_in(key, 6)
    for position, parts in split:
        draws = jnp.exp(jax.random.uniform(jax.random.fold_in(own, position), (parts,), jnp.float32, low / len(split), top_value / len(split)))
        level = level * jnp.repeat(draws, dims[position] // parts).reshape([-1 if axis == position else 1 for axis in range(len(dims))])
    return level


def gaussian(own_key, dims, spread, reach, pieces=(), held_as=jnp.bfloat16):
    entries = spread * jax.random.normal(own_key, dims, jnp.float32)
    if pieces:
        entries = entries * levels(own_key, dims, pieces, -0.22, 0.18)
    return jnp.clip(entries, -reach, reach).astype(held_as)


def setup_inputs(seed: int = 0) -> dict:
    key_list = jax.random.split(jax.random.key(seed), 7)
    return {
        "query": gaussian(key_list[0], (TOKENS, CHANNELS), 1.0, 6.0, ((0, 8), (1, 4))),
        "key": gaussian(key_list[1], (TOKENS, CHANNELS), 1.0, 6.0, ((0, 8), (1, 4))),
        "value": gaussian(key_list[2], (TOKENS, CHANNELS), 1.0, 6.0, ((0, 8), (1, 4))),
        "filter_weights": gaussian(key_list[3], (TOK_DEV, N_SEQ, CHANNELS), 1.0, 6.0, ((0, 4), (1, 8))),
        "skip_gain": jnp.clip(0.5 + 1.0 * jax.random.uniform(key_list[4], (CHANNELS,), jnp.float32) ** levels(key_list[4], (CHANNELS,), ((0, 4),), -0.2, 0.2), 0.5, 1.5),
        "cotangent": gaussian(key_list[5], (TOKENS, CHANNELS), 1.0, 6.0, ((0, 8), (1, 4))),
    }


def reference(query, key, value, filter_weights, skip_gain, cotangent):
    length = query.shape[0]
    width = query.shape[1]
    padded = 2 * length
    factor = 1.0 / math.sqrt(length)
    taps_all = filter_weights.astype(jnp.float32).transpose(1, 0, 2).reshape(length, width) * factor

    def split_groups(array_in):
        return array_in.reshape(length, N_CHAN, CH_DEV).transpose(1, 0, 2)

    def merge_groups(array_in):
        return array_in.transpose(1, 0, 2).reshape(length, N_CHAN * CH_DEV)

    def item_group(group_items):
        query_grp, key_grp, value_grp, grad_grp, gain_grp, taps_grp = group_items
        query_data = query_grp.astype(jnp.float32)
        key_data = key_grp.astype(jnp.float32)
        value_data = value_grp.astype(jnp.float32)
        grad_data = grad_grp.astype(jnp.float32)
        filter_spec = jnp.fft.rfft(taps_grp, n=padded, axis=0)
        mixed_in = key_data * value_data
        spec_in = jnp.fft.rfft(mixed_in, n=padded, axis=0)
        conv_out = jnp.fft.irfft(filter_spec * spec_in, n=padded, axis=0)[:length]
        state = conv_out + gain_grp[None, :] * mixed_in
        gate_grad = grad_data * query_data
        spec_grad = jnp.fft.rfft(gate_grad, n=padded, axis=0)
        back_grad = jnp.fft.irfft(jnp.conj(filter_spec) * spec_grad, n=padded, axis=0)[:length]
        back_grad = back_grad + gain_grp[None, :] * gate_grad
        filter_part = jnp.fft.irfft(jnp.conj(spec_in) * spec_grad, n=padded, axis=0)[:length]
        return ((query_data * state).astype(jnp.bfloat16), (grad_data * state).astype(jnp.bfloat16), (back_grad * value_data).astype(jnp.bfloat16), (back_grad * key_data).astype(jnp.bfloat16), filter_part * factor)
    gains = skip_gain.reshape(N_CHAN, CH_DEV)
    results = lax.map(item_group, (split_groups(query), split_groups(key), split_groups(value), split_groups(cotangent), gains, split_groups(taps_all)))
    filter_grad = merge_groups(results[4]).reshape(N_SEQ, length // N_SEQ, width).transpose(1, 0, 2)
    return (merge_groups(results[0]), merge_groups(results[1]), merge_groups(results[2]), merge_groups(results[3]), filter_grad)
```

```python
import functools
import math

import jax
import jax.numpy as jnp
import numpy as np
from jax import lax
from jax.experimental import pallas as pl
from jax.experimental.pallas import tpu as pltpu
from jax.sharding import PartitionSpec as P

MESH = pl.DeviceIdType.MESH
F32 = jnp.float32
BF16 = jnp.bfloat16


def whole_vmem(count):
    return [pl.BlockSpec(memory_space=pltpu.VMEM)] * count


def split_table(table):
    high = jnp.asarray(table, F32).astype(BF16)
    low = (jnp.asarray(table, F32) - high.astype(F32)).astype(BF16)
    return high, low


def split_value(x):
    high = x.astype(BF16)
    return high, (x - high.astype(F32)).astype(BF16)


def dot(a, b):
    return jnp.dot(a, b, preferred_element_type=F32)


def tables(slow, fast, factor):
    length = 2 * slow * fast
    kept = slow + 1
    padded = -(-kept // 8) * 8
    k1 = np.arange(kept)
    n1 = np.arange(slow)
    n2 = np.arange(fast)
    angle1 = 2.0 * np.pi * (np.outer(k1, n1) % (2 * slow)) / (2 * slow)
    first = np.zeros((2 * padded, slow))
    first[:kept] = np.cos(angle1)
    first[padded : padded + kept] = -np.sin(angle1)
    angle2 = 2.0 * np.pi * (np.outer(k1, n2) % length) / length
    twiddle = np.zeros((2, padded, fast))
    twiddle[0, :kept] = np.cos(angle2)
    twiddle[1, :kept] = -np.sin(angle2)
    angle3 = 2.0 * np.pi * (np.outer(n2, n2) % fast) / fast
    cosine, sine = np.cos(angle3), np.sin(angle3)
    ahead = np.block([[cosine, -sine], [sine, cosine]])
    back = np.block([[cosine, sine], [-sine, cosine]])
    weight = np.where((k1 == 0) | (k1 == slow), 1.0, 2.0)[:, None] * (factor / length)
    last = np.zeros((slow, 2 * padded))
    last[:, :kept] = (weight * np.cos(angle1)).T
    last[:, padded : padded + kept] = (-weight * np.sin(angle1)).T
    return padded, first, twiddle, ahead, back, last


def before_kernel(q_ref, k_ref, v_ref, g_ref, w_ref, sig_ref, tap_ref):
    seq_parts, _, pieces, group, fast = sig_ref.shape
    for u in range(pieces):
        rows = pl.ds(u * fast, fast)
        mixed_in = k_ref[rows, :].astype(F32) * v_ref[rows, :].astype(F32)
        gate_grad = g_ref[rows, :].astype(F32) * q_ref[rows, :].astype(F32)
        for slot, part in enumerate((mixed_in, gate_grad)):
            turned = part.T
            for t in range(seq_parts):
                sig_ref[t, slot, u] = turned[t * group : (t + 1) * group].astype(BF16)
    width = seq_parts * group
    for a in range(w_ref.shape[1] // width):
        turned = w_ref[:, a * width : (a + 1) * width].astype(F32).T
        for t in range(seq_parts):
            tap_ref[a * seq_parts + t] = turned[t * group : (t + 1) * group].astype(BF16)


def exchange_kernel(
    n_chan, n_seq, to_taps, sig_ref, tap_ref, out_sig, out_tap, own_sem, s_send, s_recv, t_send, t_recv
):
    a, s = lax.axis_index("chan"), lax.axis_index("seq")
    n_all = n_chan * n_seq
    me = a * n_seq + s

    def place(index):
        return index // n_seq, index % n_seq

    def signal_id(index):
        return index

    def block_id(index):
        chan, seq = place(index)
        return seq * n_chan + chan

    source_slot, landing_slot = (signal_id, block_id) if to_taps else (block_id, signal_id)

    barrier = pltpu.get_barrier_semaphore()

    def greet(d, carry):
        pl.semaphore_signal(
            barrier, inc=1, device_id=place(lax.rem(me + d, n_all)), device_id_type=MESH
        )
        return carry

    lax.fori_loop(1, n_all, greet, 0)
    own_sig = pltpu.make_async_copy(sig_ref.at[s], out_sig.at[s], own_sem.at[0])
    own_tap = pltpu.make_async_copy(
        tap_ref.at[source_slot(me)], out_tap.at[landing_slot(me)], own_sem.at[1]
    )
    own_sig.start()
    own_tap.start()
    pl.semaphore_wait(barrier, n_all - 1)

    def sig_copy(d, landing):
        there = lax.rem(s + d, n_seq)
        return pltpu.make_async_remote_copy(
            src_ref=sig_ref.at[there],
            dst_ref=out_sig.at[landing],
            send_sem=s_send.at[d],
            recv_sem=s_recv.at[d],
            device_id=(a, there),
            device_id_type=MESH,
        )

    def tap_copy(d, landing):
        there = lax.rem(me + d, n_all)
        return pltpu.make_async_remote_copy(
            src_ref=tap_ref.at[source_slot(there)],
            dst_ref=out_tap.at[landing],
            send_sem=t_send.at[d],
            recv_sem=t_recv.at[d],
            device_id=place(there),
            device_id_type=MESH,
        )

    def start_sig(d, carry):
        sig_copy(d, s).start()
        return carry

    def start_tap(d, carry):
        tap_copy(d, landing_slot(me)).start()
        return carry

    lax.fori_loop(1, n_seq, start_sig, 0)
    lax.fori_loop(1, n_all, start_tap, 0)

    def wait_sig(d, carry):
        sig_copy(d, lax.rem(s + n_seq - d, n_seq)).wait()
        return carry

    def wait_tap(d, carry):
        tap_copy(d, landing_slot(lax.rem(me + n_all - d, n_all))).wait()
        return carry

    own_sig.wait()
    own_tap.wait()
    lax.fori_loop(1, n_seq, wait_sig, 0)
    lax.fori_loop(1, n_all, wait_tap, 0)


def exchange(n_chan, n_seq, to_taps, sig, taps):
    n_all = n_chan * n_seq
    return pl.pallas_call(
        functools.partial(exchange_kernel, n_chan, n_seq, to_taps),
        out_shape=[
            jax.ShapeDtypeStruct(sig.shape, sig.dtype),
            jax.ShapeDtypeStruct(taps.shape, taps.dtype),
        ],
        in_specs=whole_vmem(2),
        out_specs=whole_vmem(2),
        scratch_shapes=[
            pltpu.SemaphoreType.DMA((2,)),
            pltpu.SemaphoreType.DMA((n_seq,)),
            pltpu.SemaphoreType.DMA((n_seq,)),
            pltpu.SemaphoreType.DMA((n_all,)),
            pltpu.SemaphoreType.DMA((n_all,)),
        ],
        compiler_params=pltpu.CompilerParams(
            collective_id=0 if to_taps else 1, has_side_effects=True
        ),
        name="spread" if to_taps else "collect",
    )(sig, taps)


def conv_kernel(
    padded, sig_ref, tap_ref, first_h, first_l, twid_ref, ahead_h, ahead_l, back_h, back_l, last_h, last_l,
    out_sig, out_tap, lines, turned, spec,
):
    seq_parts, _, pieces, group, fast = sig_ref.shape
    slow = seq_parts * pieces
    for s in range(seq_parts):
        for u in range(pieces):
            row = s * pieces + u
            at = pl.ds(row * group, group)
            lines[0, at, :] = sig_ref[s, 0, u].astype(F32)
            lines[1, at, :] = sig_ref[s, 1, u].astype(F32)
            lines[2, at, :] = tap_ref[row].astype(F32)
    cosine, sine = twid_ref[0], twid_ref[1]
    for slot in range(3):
        for c in range(group):
            column = lines[slot, pl.ds(c, slow, stride=group), :].astype(BF16)
            got = dot(first_h[...], column) + dot(first_l[...], column)
            real, imag = got[:padded], got[padded:]
            at = pl.ds(c * padded, padded)
            turned[slot, at, :fast] = real * cosine - imag * sine
            turned[slot, at, fast:] = real * sine + imag * cosine

    def through(x, high, low):
        x_high, x_low = split_value(x)
        return dot(x_high, high[...]) + dot(x_low, high[...]) + dot(x_high, low[...])

    for c in range(group):
        at = pl.ds(c * padded, padded)
        lists = []
        for slot in range(3):
            line = through(turned[slot, at, :], ahead_h, ahead_l)
            lists.append((line[:, :fast], line[:, fast:]))
        (xr, xi), (gr, gi), (fr, fi) = lists
        spec[0, at, :fast] = fr * xr - fi * xi
        spec[0, at, fast:] = fr * xi + fi * xr
        spec[1, at, :fast] = fr * gr + fi * gi
        spec[1, at, fast:] = fr * gi - fi * gr
        spec[2, at, :fast] = xr * gr + xi * gi
        spec[2, at, fast:] = xr * gi - xi * gr
    for c in range(group):
        at = pl.ds(c * padded, padded)
        for slot in range(3):
            line = through(spec[slot, at, :], back_h, back_l)
            real, imag = line[:, :fast], line[:, fast:]
            both = jnp.concatenate(
                [real * cosine + imag * sine, imag * cosine - real * sine], axis=0
            )
            both_h, both_l = split_value(both)
            lines[slot, pl.ds(c, slow, stride=group), :] = (
                dot(last_h[...], both_h) + dot(last_h[...], both_l) + dot(last_l[...], both_h)
            )
    for s in range(seq_parts):
        for u in range(pieces):
            row = s * pieces + u
            at = pl.ds(row * group, group)
            out_sig[s, 0, u] = lines[0, at, :].astype(BF16)
            out_sig[s, 1, u] = lines[1, at, :].astype(BF16)
            out_tap[row] = lines[2, at, :].astype(BF16)


def after_kernel(
    q_ref, k_ref, v_ref, g_ref, gain_ref, sig_ref, tap_ref, m_ref, qg_ref, kg_ref, vg_ref, fg_ref, hold
):
    seq_parts, _, pieces, group, fast = sig_ref.shape
    width = seq_parts * group
    gain = gain_ref[...]

    def columns(pick):
        for t in range(seq_parts):
            hold[pl.ds(t * group, group), :] = pick(t).astype(F32)
        return hold[...].T

    for u in range(pieces):
        rows = pl.ds(u * fast, fast)
        query, key = q_ref[rows, :].astype(F32), k_ref[rows, :].astype(F32)
        value, grad = v_ref[rows, :].astype(F32), g_ref[rows, :].astype(F32)
        state = columns(lambda t: sig_ref[t, 0, u]) + gain * (key * value)
        m_ref[rows, :] = (query * state).astype(BF16)
        qg_ref[rows, :] = (grad * state).astype(BF16)
        back = columns(lambda t: sig_ref[t, 1, u]) + gain * (grad * query)
        kg_ref[rows, :] = (back * value).astype(BF16)
        vg_ref[rows, :] = (back * key).astype(BF16)
    for a in range(tap_ref.shape[0] // seq_parts):
        fg_ref[:, a * width : (a + 1) * width] = columns(lambda t: tap_ref[a * seq_parts + t])


def body(n_chan, n_seq, query, key, value, filter_weights, skip_gain, cotangent):
    rows, width = query.shape
    tap_rows, _, all_width = filter_weights.shape
    fast, group, pieces, n_all = tap_rows, width // n_seq, n_chan, n_chan * n_seq
    slow = rows * n_seq // fast
    padded, first, twiddle, ahead, back, last = tables(slow, fast, 1.0 / math.sqrt(rows * n_seq))
    weights = filter_weights.reshape(tap_rows, all_width)
    sig_shape = jax.ShapeDtypeStruct((n_seq, 2, pieces, group, fast), BF16)
    tap_shape = jax.ShapeDtypeStruct((n_all, group, fast), BF16)
    limit = pltpu.CompilerParams(vmem_limit_bytes=60 * 1024 * 1024)
    sig, taps = pl.pallas_call(
        before_kernel,
        out_shape=[sig_shape, tap_shape],
        in_specs=whole_vmem(5),
        out_specs=whole_vmem(2),
        compiler_params=limit,
        name="before",
    )(query, key, value, cotangent, weights)
    sig, taps = exchange(n_chan, n_seq, True, sig, taps)
    consts = [*split_table(first), jnp.asarray(twiddle, F32)]
    for table in (ahead, back, last):
        consts += split_table(table)
    sig, taps = pl.pallas_call(
        functools.partial(conv_kernel, padded),
        out_shape=[sig_shape, tap_shape],
        in_specs=whole_vmem(2 + len(consts)),
        out_specs=whole_vmem(2),
        scratch_shapes=[
            pltpu.VMEM((3, slow * group, fast), F32),
            pltpu.VMEM((3, group * padded, 2 * fast), F32),
            pltpu.VMEM((3, group * padded, 2 * fast), F32),
        ],
        compiler_params=limit,
        name="conv",
    )(sig, taps, *consts)
    sig, taps = exchange(n_chan, n_seq, False, sig, taps)
    flat = jax.ShapeDtypeStruct((rows, width), BF16)
    outs = pl.pallas_call(
        after_kernel,
        out_shape=[flat, flat, flat, flat, jax.ShapeDtypeStruct((tap_rows, all_width), F32)],
        in_specs=whole_vmem(7),
        out_specs=whole_vmem(5),
        scratch_shapes=[pltpu.VMEM((width, fast), F32)],
        compiler_params=limit,
        name="after",
    )(query, key, value, cotangent, skip_gain.reshape(1, width), sig, taps)
    return (*outs[:4], outs[4].reshape(tap_rows, 1, all_width))


def solution(mesh):
    n_chan, n_seq = mesh.shape["chan"], mesh.shape["seq"]
    block = P("seq", "chan")
    taps = P("chan", "seq", None)
    return jax.shard_map(
        functools.partial(body, n_chan, n_seq),
        mesh=mesh,
        in_specs=(block, block, block, taps, P("chan"), block),
        out_specs=(block, block, block, block, taps),
        check_vma=False,
    )
```

```python
import functools
import math

import jax
import jax.numpy as jnp
import numpy as np
from jax import lax
from jax.experimental import pallas as pl
from jax.experimental.pallas import tpu as pltpu
from jax.sharding import PartitionSpec as P

MESH = pl.DeviceIdType.MESH
F32 = jnp.float32
BF16 = jnp.bfloat16


def whole_vmem(count):
    return [pl.BlockSpec(memory_space=pltpu.VMEM)] * count


def split_table(table):
    high = jnp.asarray(table, F32).astype(BF16)
    low = (jnp.asarray(table, F32) - high.astype(F32)).astype(BF16)
    return high, low


def dot(a, b):
    return jnp.dot(a, b, preferred_element_type=F32)


def tables(slow, fast, factor):
    length = 2 * slow * fast
    kept = slow + 1
    padded = -(-kept // 8) * 8
    k1 = np.arange(kept)
    n1 = np.arange(slow)
    n2 = np.arange(fast)
    angle1 = 2.0 * np.pi * (np.outer(k1, n1) % (2 * slow)) / (2 * slow)
    first = np.zeros((2 * padded, slow))
    first[:kept] = np.cos(angle1)
    first[padded : padded + kept] = -np.sin(angle1)
    angle2 = 2.0 * np.pi * (np.outer(k1, n2) % length) / length
    twiddle = np.zeros((2, padded, fast))
    twiddle[0, :kept] = np.cos(angle2)
    twiddle[1, :kept] = -np.sin(angle2)
    angle3 = 2.0 * np.pi * (np.outer(n2, n2) % fast) / fast
    cosine, sine = np.cos(angle3), np.sin(angle3)
    ahead = np.block([[cosine, -sine], [sine, cosine]])
    back = np.block([[cosine, sine], [-sine, cosine]])
    weight = np.where((k1 == 0) | (k1 == slow), 1.0, 2.0)[:, None] * (factor / length)
    last = np.zeros((slow, 2 * padded))
    last[:, :kept] = (weight * np.cos(angle1)).T
    last[:, padded : padded + kept] = (-weight * np.sin(angle1)).T
    return padded, first, twiddle, ahead, back, last


def core_kernel(
    n_chan, n_seq, padded,
    q_ref, k_ref, v_ref, g_ref, w_ref, first_ref, twid_ref, ahead_h, ahead_l, back_h, back_l, last_ref,
    out_sig, out_tap,
    send_sig, send_tap, in_sig, in_tap, res_sig, res_tap, lines, turned, spec,
    own_sem, s_send, s_recv, t_send, t_recv, rs_send, rs_recv, rt_send, rt_recv,
):
    chan, seq = lax.axis_index("chan"), lax.axis_index("seq")
    n_all = n_chan * n_seq
    me = chan * n_seq + seq
    _, chunks, _, pieces, part, fast = send_sig.shape
    group = chunks * part
    slow = n_seq * pieces
    width = n_seq * group

    def place(index):
        return index // n_seq, index % n_seq

    def block_of(index):
        at_chan, at_seq = place(index)
        return at_seq * n_chan + at_chan

    barrier = pltpu.get_barrier_semaphore()

    def greet(d, carry):
        pl.semaphore_signal(
            barrier, inc=1, device_id=place(lax.rem(me + d, n_all)), device_id_type=MESH
        )
        return carry

    lax.fori_loop(1, n_all, greet, 0)

    for u in range(pieces):
        rows = pl.ds(u * fast, fast)
        mixed_in = k_ref[rows, :].astype(F32) * v_ref[rows, :].astype(F32)
        gate_grad = g_ref[rows, :].astype(F32) * q_ref[rows, :].astype(F32)
        for slot, signal in enumerate((mixed_in, gate_grad)):
            flipped = signal.T
            for t in range(n_seq):
                for q in range(chunks):
                    low = t * group + q * part
                    send_sig[t, q, slot, u] = flipped[low : low + part].astype(BF16)
    for a in range(n_chan):
        flipped = w_ref[:, a * width : (a + 1) * width].astype(F32).T
        for t in range(n_seq):
            send_tap[a * n_seq + t] = flipped[t * group : (t + 1) * group].astype(BF16)

    def remote(source, target, send, recv, device):
        return pltpu.make_async_remote_copy(
            src_ref=source, dst_ref=target, send_sem=send, recv_sem=recv,
            device_id=device, device_id_type=MESH,
        )

    def sig_copy(q, d, landing, ahead):
        there = lax.rem(seq + d, n_seq)
        source, target = (send_sig, in_sig) if ahead else (res_sig, out_sig)
        send, recv = (s_send, s_recv) if ahead else (rs_send, rs_recv)
        return remote(
            source.at[there, q], target.at[landing, q], send.at[q, d], recv.at[q, d], (chan, there)
        )

    def tap_copy(d, landing):
        there = lax.rem(me + d, n_all)
        return remote(
            send_tap.at[there], in_tap.at[landing], t_send.at[d], t_recv.at[d], place(there)
        )

    def grad_copy(q, d, landing):
        there = lax.rem(me + d, n_all)
        return remote(
            res_tap.at[q, block_of(there)], out_tap.at[q, landing],
            rt_send.at[q, d], rt_recv.at[q, d], place(there),
        )

    def each(count, act):
        def step(d, carry):
            act(d)
            return carry

        lax.fori_loop(1, count, step, 0)

    def seq_from(d):
        return lax.rem(seq + n_seq - d, n_seq)

    def all_from(d):
        return lax.rem(me + n_all - d, n_all)

    own = [pltpu.make_async_copy(send_tap.at[me], in_tap.at[block_of(me)], own_sem.at[0])]
    for q in range(chunks):
        own.append(
            pltpu.make_async_copy(send_sig.at[seq, q], in_sig.at[seq, q], own_sem.at[1 + q])
        )

    pl.semaphore_wait(barrier, n_all - 1)
    each(n_seq, lambda d: sig_copy(0, d, seq, True).start())
    each(n_all, lambda d: tap_copy(d, block_of(me)).start())
    for q in range(1, chunks):
        each(n_seq, lambda d: sig_copy(q, d, seq, True).start())
    for copy in own:
        copy.start()

    cosine, sine = twid_ref[0], twid_ref[1]
    joint = fast % 128 == 0 and part % 2 == 0
    batch = 2 if joint else 1

    def times(table, columns):
        if not joint:
            return [dot(table, column) for column in columns]
        wide = dot(table, jnp.concatenate(columns, axis=1))
        return [wide[:, i * fast : (i + 1) * fast] for i in range(len(columns))]

    def through(x, high, low):
        short = x.astype(BF16)
        return dot(short, high[...]) + dot(short, low[...])

    def transform(q):
        for s in range(n_seq):
            for u in range(pieces):
                row = s * pieces + u
                at = pl.ds(row * part, part)
                lines[0, at, :] = in_sig[s, q, 0, u].astype(F32)
                lines[1, at, :] = in_sig[s, q, 1, u].astype(F32)
                lines[2, at, :] = in_tap[row, q * part : (q + 1) * part].astype(F32)
        for base in range(0, part, batch):
            picks = [(slot, c) for c in range(base, base + batch) for slot in range(3)]
            columns = []
            for slot, c in picks:
                column = lines[slot, pl.ds(c, slow, stride=part), :].astype(BF16)
                columns.append(jnp.concatenate([column, column], axis=0))
            for (slot, c), got in zip(picks, times(first_ref[...], columns)):
                real, imag = got[:padded], got[padded:]
                at = pl.ds(c * padded, padded)
                turned[slot, at, :fast] = real * cosine - imag * sine
                turned[slot, at, fast:] = real * sine + imag * cosine
        for slot in range(3):
            turned[slot] = through(turned[slot], ahead_h, ahead_l)
        for c in range(part):
            at = pl.ds(c * padded, padded)
            xr, xi = turned[0, at, :fast], turned[0, at, fast:]
            gr, gi = turned[1, at, :fast], turned[1, at, fast:]
            fr, fi = turned[2, at, :fast], turned[2, at, fast:]
            spec[0, at, :fast] = fr * xr - fi * xi
            spec[0, at, fast:] = fr * xi + fi * xr
            spec[1, at, :fast] = fr * gr + fi * gi
            spec[1, at, fast:] = fr * gi - fi * gr
            spec[2, at, :fast] = xr * gr + xi * gi
            spec[2, at, fast:] = xr * gi - xi * gr
        for slot in range(3):
            spec[slot] = through(spec[slot], back_h, back_l)
        for base in range(0, part, batch):
            picks = [(slot, c) for c in range(base, base + batch) for slot in range(3)]
            columns = []
            for slot, c in picks:
                at = pl.ds(c * padded, padded)
                real, imag = spec[slot, at, :fast], spec[slot, at, fast:]
                real, imag = real * cosine + imag * sine, imag * cosine - real * sine
                both = jnp.concatenate([real, imag], axis=0).astype(BF16)
                columns.append(jnp.concatenate([both, both], axis=0))
            for (slot, c), got in zip(picks, times(last_ref[...], columns)):
                lines[slot, pl.ds(c, slow, stride=part), :] = got
        for s in range(n_seq):
            for u in range(pieces):
                row = s * pieces + u
                at = pl.ds(row * part, part)
                res_sig[s, q, 0, u] = lines[0, at, :].astype(BF16)
                res_sig[s, q, 1, u] = lines[1, at, :].astype(BF16)
                res_tap[q, row] = lines[2, at, :].astype(BF16)

    own[0].wait()
    for q in range(chunks):
        own[1 + q].wait()
        each(n_seq, lambda d: sig_copy(q, d, seq_from(d), True).wait())
        if q == 0:
            each(n_all, lambda d: tap_copy(d, block_of(all_from(d))).wait())
        transform(q)
        each(n_seq, lambda d: sig_copy(q, d, seq, False).start())
        each(n_all, lambda d: grad_copy(q, d, me).start())
        for copy in (
            pltpu.make_async_copy(res_sig.at[seq, q], out_sig.at[seq, q], own_sem.at[1 + chunks + q]),
            pltpu.make_async_copy(
                res_tap.at[q, block_of(me)], out_tap.at[q, me], own_sem.at[1 + 2 * chunks + q]
            ),
        ):
            copy.start()
            own.append(copy)
    for copy in own[1 + chunks :]:
        copy.wait()
    for q in range(chunks):
        each(n_seq, lambda d: sig_copy(q, d, seq_from(d), False).wait())
        each(n_all, lambda d: grad_copy(q, d, all_from(d)).wait())


def after_kernel(
    q_ref, k_ref, v_ref, g_ref, gain_ref, sig_ref, tap_ref, m_ref, qg_ref, kg_ref, vg_ref, fg_ref, hold
):
    seq_parts, chunks, _, pieces, part, fast = sig_ref.shape
    group = chunks * part
    gain = gain_ref[...]

    def columns(pick):
        for t in range(seq_parts):
            for q in range(chunks):
                hold[pl.ds(t * group + q * part, part), :] = pick(t, q).astype(F32)
        return hold[...].T

    for u in range(pieces):
        rows = pl.ds(u * fast, fast)
        query, key = q_ref[rows, :].astype(F32), k_ref[rows, :].astype(F32)
        value, grad = v_ref[rows, :].astype(F32), g_ref[rows, :].astype(F32)
        state = columns(lambda t, q: sig_ref[t, q, 0, u]) + gain * (key * value)
        m_ref[rows, :] = (query * state).astype(BF16)
        qg_ref[rows, :] = (grad * state).astype(BF16)
        back = columns(lambda t, q: sig_ref[t, q, 1, u]) + gain * (grad * query)
        kg_ref[rows, :] = (back * value).astype(BF16)
        vg_ref[rows, :] = (back * key).astype(BF16)
    for a in range(pieces):
        got = columns(lambda t, q: tap_ref[q, a * seq_parts + t])
        fg_ref[pl.ds(a, fast, stride=pieces), :] = got


def body(n_chan, n_seq, query, key, value, filter_weights, skip_gain, cotangent):
    rows, width = query.shape
    tap_rows, _, all_width = filter_weights.shape
    fast, group, pieces, n_all = tap_rows, width // n_seq, n_chan, n_chan * n_seq
    slow = rows * n_seq // fast
    chunks = 2 if group % 16 == 0 else 1
    part = group // chunks
    padded, first, twiddle, ahead, back, last = tables(slow, fast, 1.0 / math.sqrt(rows * n_seq))
    weights = filter_weights.reshape(tap_rows, all_width)
    consts = [
        jnp.concatenate(split_table(first), axis=1),
        jnp.asarray(twiddle, F32),
        *split_table(ahead),
        *split_table(back),
        jnp.concatenate(split_table(last), axis=1),
    ]
    sig_dims = (n_seq, chunks, 2, pieces, part, fast)
    grad_dims = (chunks, n_all, part, fast)
    tap_dims = (n_all, group, fast)
    dma = pltpu.SemaphoreType.DMA
    sig, taps = pl.pallas_call(
        functools.partial(core_kernel, n_chan, n_seq, padded),
        out_shape=[jax.ShapeDtypeStruct(sig_dims, BF16), jax.ShapeDtypeStruct(grad_dims, BF16)],
        in_specs=whole_vmem(5 + len(consts)),
        out_specs=whole_vmem(2),
        scratch_shapes=[
            pltpu.VMEM(sig_dims, BF16),
            pltpu.VMEM(tap_dims, BF16),
            pltpu.VMEM(sig_dims, BF16),
            pltpu.VMEM(tap_dims, BF16),
            pltpu.VMEM(sig_dims, BF16),
            pltpu.VMEM(grad_dims, BF16),
            pltpu.VMEM((3, slow * part, fast), F32),
            pltpu.VMEM((3, part * padded, 2 * fast), F32),
            pltpu.VMEM((3, part * padded, 2 * fast), F32),
            dma((1 + 3 * chunks,)),
            dma((chunks, n_seq)),
            dma((chunks, n_seq)),
            dma((n_all,)),
            dma((n_all,)),
            dma((chunks, n_seq)),
            dma((chunks, n_seq)),
            dma((chunks, n_all)),
            dma((chunks, n_all)),
        ],
        compiler_params=pltpu.CompilerParams(
            collective_id=0, has_side_effects=True, vmem_limit_bytes=60 * 1024 * 1024
        ),
        name="core",
    )(query, key, value, cotangent, weights, *consts)
    flat = jax.ShapeDtypeStruct((rows, width), BF16)
    outs = pl.pallas_call(
        after_kernel,
        out_shape=[flat, flat, flat, flat, jax.ShapeDtypeStruct((tap_rows * n_chan, width), F32)],
        in_specs=whole_vmem(7),
        out_specs=whole_vmem(5),
        scratch_shapes=[pltpu.VMEM((width, fast), F32)],
        compiler_params=pltpu.CompilerParams(vmem_limit_bytes=60 * 1024 * 1024),
        name="after",
    )(query, key, value, cotangent, skip_gain.reshape(1, width), sig, taps)
    return (*outs[:4], outs[4].reshape(tap_rows, 1, all_width))


def solution(mesh):
    n_chan, n_seq = mesh.shape["chan"], mesh.shape["seq"]
    block = P("seq", "chan")
    taps = P("chan", "seq", None)
    return jax.shard_map(
        functools.partial(body, n_chan, n_seq),
        mesh=mesh,
        in_specs=(block, block, block, taps, P("chan"), block),
        out_specs=(block, block, block, block, taps),
        check_vma=False,
    )
```

```python
import functools
import math

import jax
import jax.numpy as jnp
import numpy as np
from jax import lax
from jax.experimental import pallas as pl
from jax.experimental.pallas import tpu as pltpu
from jax.sharding import PartitionSpec as P

MESH = pl.DeviceIdType.MESH
F32 = jnp.float32
BF16 = jnp.bfloat16


def whole_vmem(count):
    return [pl.BlockSpec(memory_space=pltpu.VMEM)] * count


def split_table(table):
    high = jnp.asarray(table, F32).astype(BF16)
    low = (jnp.asarray(table, F32) - high.astype(F32)).astype(BF16)
    return high, low


def dot(a, b):
    return jnp.dot(a, b, preferred_element_type=F32)


def tables(slow, fast, factor):
    length = 2 * slow * fast
    kept = slow + 1
    padded = -(-kept // 8) * 8
    k1 = np.arange(kept)
    n1 = np.arange(slow)
    n2 = np.arange(fast)
    angle1 = 2.0 * np.pi * (np.outer(k1, n1) % (2 * slow)) / (2 * slow)
    first = np.zeros((2 * padded, slow))
    first[:kept] = np.cos(angle1)
    first[padded : padded + kept] = -np.sin(angle1)
    angle2 = 2.0 * np.pi * (np.outer(k1, n2) % length) / length
    twiddle = np.zeros((2, padded, fast))
    twiddle[0, :kept] = np.cos(angle2)
    twiddle[1, :kept] = -np.sin(angle2)
    angle3 = 2.0 * np.pi * (np.outer(n2, n2) % fast) / fast
    cosine, sine = np.cos(angle3), np.sin(angle3)
    ahead = np.block([[cosine, -sine], [sine, cosine]])
    back = np.block([[cosine, sine], [-sine, cosine]])
    weight = np.where((k1 == 0) | (k1 == slow), 1.0, 2.0)[:, None] * (factor / length)
    last = np.zeros((slow, 2 * padded))
    last[:, :kept] = (weight * np.cos(angle1)).T
    last[:, padded : padded + kept] = (-weight * np.sin(angle1)).T
    return padded, first, twiddle, ahead, back, last


def core_kernel(
    n_chan, n_seq, padded,
    q_ref, k_ref, v_ref, g_ref, w_ref, first_ref, twid_ref, ahead_h, ahead_l, back_h, back_l, last_ref,
    out_sig, out_tap,
    send_sig, send_tap, in_sig, in_tap, res_sig, res_tap, lines, turned, spec,
    own_sem, s_send, s_recv, t_send, t_recv, rs_send, rs_recv, rt_send, rt_recv,
):
    chan, seq = lax.axis_index("chan"), lax.axis_index("seq")
    n_all = n_chan * n_seq
    me = chan * n_seq + seq
    _, chunks, _, pieces, part, fast = send_sig.shape
    group = chunks * part
    slow = n_seq * pieces
    width = n_seq * group

    def place(index):
        return index // n_seq, index % n_seq

    def block_of(index):
        at_chan, at_seq = place(index)
        return at_seq * n_chan + at_chan

    barrier = pltpu.get_barrier_semaphore()

    def greet(d, carry):
        pl.semaphore_signal(
            barrier, inc=1, device_id=place(lax.rem(me + d, n_all)), device_id_type=MESH
        )
        return carry

    lax.fori_loop(1, n_all, greet, 0)

    for u in range(pieces):
        rows = pl.ds(u * fast, fast)
        mixed_in = k_ref[rows, :].astype(F32) * v_ref[rows, :].astype(F32)
        gate_grad = g_ref[rows, :].astype(F32) * q_ref[rows, :].astype(F32)
        for slot, signal in enumerate((mixed_in, gate_grad)):
            flipped = signal.T
            for t in range(n_seq):
                for q in range(chunks):
                    low = t * group + q * part
                    send_sig[t, q, slot, u] = flipped[low : low + part].astype(BF16)
    for a in range(n_chan):
        flipped = w_ref[:, a * width : (a + 1) * width].astype(F32).T
        for t in range(n_seq):
            send_tap[a * n_seq + t] = flipped[t * group : (t + 1) * group].astype(BF16)

    def remote(source, target, send, recv, device):
        return pltpu.make_async_remote_copy(
            src_ref=source, dst_ref=target, send_sem=send, recv_sem=recv,
            device_id=device, device_id_type=MESH,
        )

    def sig_copy(q, d, landing, ahead):
        there = lax.rem(seq + d, n_seq)
        source, target = (send_sig, in_sig) if ahead else (res_sig, out_sig)
        send, recv = (s_send, s_recv) if ahead else (rs_send, rs_recv)
        return remote(
            source.at[there, q], target.at[landing, q], send.at[q, d], recv.at[q, d], (chan, there)
        )

    def tap_copy(d, landing):
        there = lax.rem(me + d, n_all)
        return remote(
            send_tap.at[there], in_tap.at[landing], t_send.at[d], t_recv.at[d], place(there)
        )

    def grad_copy(q, d, landing):
        there = lax.rem(me + d, n_all)
        return remote(
            res_tap.at[q, block_of(there)], out_tap.at[q, landing],
            rt_send.at[q, d], rt_recv.at[q, d], place(there),
        )

    def each(count, act):
        def step(d, carry):
            act(d)
            return carry

        lax.fori_loop(1, count, step, 0)

    def seq_from(d):
        return lax.rem(seq + n_seq - d, n_seq)

    def all_from(d):
        return lax.rem(me + n_all - d, n_all)

    own = [pltpu.make_async_copy(send_tap.at[me], in_tap.at[block_of(me)], own_sem.at[0])]
    for q in range(chunks):
        own.append(
            pltpu.make_async_copy(send_sig.at[seq, q], in_sig.at[seq, q], own_sem.at[1 + q])
        )

    pl.semaphore_wait(barrier, n_all - 1)
    each(n_seq, lambda d: sig_copy(0, d, seq, True).start())
    each(n_all, lambda d: tap_copy(d, block_of(me)).start())
    for q in range(1, chunks):
        each(n_seq, lambda d: sig_copy(q, d, seq, True).start())
    for copy in own:
        copy.start()

    cosine, sine = twid_ref[0], twid_ref[1]
    joint = fast % 128 == 0 and part % 2 == 0
    batch = 2 if joint else 1

    def times(table, columns):
        if not joint:
            return [dot(table, column) for column in columns]
        wide = dot(table, jnp.concatenate(columns, axis=1))
        return [wide[:, i * fast : (i + 1) * fast] for i in range(len(columns))]

    def through(x, high, low):
        short = x.astype(BF16)
        return dot(short, high[...]) + dot(short, low[...])

    def transform(q):
        for s in range(n_seq):
            for u in range(pieces):
                row = s * pieces + u
                at = pl.ds(row * part, part)
                lines[0, at, :] = in_sig[s, q, 0, u].astype(F32)
                lines[1, at, :] = in_sig[s, q, 1, u].astype(F32)
                lines[2, at, :] = in_tap[row, q * part : (q + 1) * part].astype(F32)
        for base in range(0, part, batch):
            picks = [(slot, c) for c in range(base, base + batch) for slot in range(3)]
            columns = []
            for slot, c in picks:
                column = lines[slot, pl.ds(c, slow, stride=part), :].astype(BF16)
                columns.append(jnp.concatenate([column, column], axis=0))
            for (slot, c), got in zip(picks, times(first_ref[...], columns)):
                real, imag = got[:padded], got[padded:]
                at = pl.ds(c * padded, padded)
                turned[slot, at, :fast] = real * cosine - imag * sine
                turned[slot, at, fast:] = real * sine + imag * cosine
        for slot in range(3):
            turned[slot] = through(turned[slot], ahead_h, ahead_l)
        for c in range(part):
            at = pl.ds(c * padded, padded)
            xr, xi = turned[0, at, :fast], turned[0, at, fast:]
            gr, gi = turned[1, at, :fast], turned[1, at, fast:]
            fr, fi = turned[2, at, :fast], turned[2, at, fast:]
            spec[0, at, :fast] = fr * xr - fi * xi
            spec[0, at, fast:] = fr * xi + fi * xr
            spec[1, at, :fast] = fr * gr + fi * gi
            spec[1, at, fast:] = fr * gi - fi * gr
            spec[2, at, :fast] = xr * gr + xi * gi
            spec[2, at, fast:] = xr * gi - xi * gr
        for slot in range(3):
            spec[slot] = through(spec[slot], back_h, back_l)
        for base in range(0, part, batch):
            picks = [(slot, c) for c in range(base, base + batch) for slot in range(3)]
            columns = []
            for slot, c in picks:
                at = pl.ds(c * padded, padded)
                real, imag = spec[slot, at, :fast], spec[slot, at, fast:]
                real, imag = real * cosine + imag * sine, imag * cosine - real * sine
                both = jnp.concatenate([real, imag], axis=0).astype(BF16)
                columns.append(jnp.concatenate([both, both], axis=0))
            for (slot, c), got in zip(picks, times(last_ref[...], columns)):
                lines[slot, pl.ds(c, slow, stride=part), :] = got
        for s in range(n_seq):
            for u in range(pieces):
                row = s * pieces + u
                at = pl.ds(row * part, part)
                res_sig[s, q, 0, u] = lines[0, at, :].astype(BF16)
                res_sig[s, q, 1, u] = lines[1, at, :].astype(BF16)
                res_tap[q, row] = lines[2, at, :].astype(BF16)

    own[0].wait()
    for q in range(chunks):
        own[1 + q].wait()
        each(n_seq, lambda d: sig_copy(q, d, seq_from(d), True).wait())
        if q == 0:
            each(n_all, lambda d: tap_copy(d, block_of(all_from(d))).wait())
        transform(q)
        each(n_seq, lambda d: sig_copy(q, d, seq, False).start())
        each(n_all, lambda d: grad_copy(q, d, me).start())
        for copy in (
            pltpu.make_async_copy(res_sig.at[seq, q], out_sig.at[seq, q], own_sem.at[1 + chunks + q]),
            pltpu.make_async_copy(
                res_tap.at[q, block_of(me)], out_tap.at[q, me], own_sem.at[1 + 2 * chunks + q]
            ),
        ):
            copy.start()
            own.append(copy)
    for copy in own[1 + chunks :]:
        copy.wait()
    for q in range(chunks):
        each(n_seq, lambda d: sig_copy(q, d, seq_from(d), False).wait())
        each(n_all, lambda d: grad_copy(q, d, all_from(d)).wait())


def after_kernel(
    q_ref, k_ref, v_ref, g_ref, gain_ref, sig_ref, tap_ref, m_ref, qg_ref, kg_ref, vg_ref, fg_ref, hold
):
    seq_parts, chunks, _, pieces, part, fast = sig_ref.shape
    group = chunks * part
    gain = gain_ref[...]

    def columns(pick):
        for t in range(seq_parts):
            for q in range(chunks):
                hold[pl.ds(t * group + q * part, part), :] = pick(t, q).astype(F32)
        return hold[...].T

    for u in range(pieces):
        rows = pl.ds(u * fast, fast)
        query, key = q_ref[rows, :].astype(F32), k_ref[rows, :].astype(F32)
        value, grad = v_ref[rows, :].astype(F32), g_ref[rows, :].astype(F32)
        state = columns(lambda t, q: sig_ref[t, q, 0, u]) + gain * (key * value)
        m_ref[rows, :] = (query * state).astype(BF16)
        qg_ref[rows, :] = (grad * state).astype(BF16)
        back = columns(lambda t, q: sig_ref[t, q, 1, u]) + gain * (grad * query)
        kg_ref[rows, :] = (back * value).astype(BF16)
        vg_ref[rows, :] = (back * key).astype(BF16)
    for a in range(pieces):
        got = columns(lambda t, q: tap_ref[q, a * seq_parts + t])
        fg_ref[pl.ds(a, fast, stride=pieces), :] = got


def body(n_chan, n_seq, query, key, value, filter_weights, skip_gain, cotangent):
    rows, width = query.shape
    tap_rows, _, all_width = filter_weights.shape
    fast, group, pieces, n_all = tap_rows, width // n_seq, n_chan, n_chan * n_seq
    slow = rows * n_seq // fast
    chunks = 2 if group % 16 == 0 else 1
    part = group // chunks
    padded, first, twiddle, ahead, back, last = tables(slow, fast, 1.0 / math.sqrt(rows * n_seq))
    weights = filter_weights.reshape(tap_rows, all_width)
    consts = [
        jnp.concatenate(split_table(first), axis=1),
        jnp.asarray(twiddle, F32),
        *split_table(ahead),
        *split_table(back),
        jnp.concatenate(split_table(last), axis=1),
    ]
    sig_dims = (n_seq, chunks, 2, pieces, part, fast)
    grad_dims = (chunks, n_all, part, fast)
    tap_dims = (n_all, group, fast)
    dma = pltpu.SemaphoreType.DMA
    sig, taps = pl.pallas_call(
        functools.partial(core_kernel, n_chan, n_seq, padded),
        out_shape=[pltpu.VMEM(sig_dims, BF16), pltpu.VMEM(grad_dims, BF16)],
        in_specs=whole_vmem(5 + len(consts)),
        out_specs=whole_vmem(2),
        scratch_shapes=[
            pltpu.VMEM(sig_dims, BF16),
            pltpu.VMEM(tap_dims, BF16),
            pltpu.VMEM(sig_dims, BF16),
            pltpu.VMEM(tap_dims, BF16),
            pltpu.VMEM(sig_dims, BF16),
            pltpu.VMEM(grad_dims, BF16),
            pltpu.VMEM((3, slow * part, fast), F32),
            pltpu.VMEM((3, part * padded, 2 * fast), F32),
            pltpu.VMEM((3, part * padded, 2 * fast), F32),
            dma((1 + 3 * chunks,)),
            dma((chunks, n_seq)),
            dma((chunks, n_seq)),
            dma((n_all,)),
            dma((n_all,)),
            dma((chunks, n_seq)),
            dma((chunks, n_seq)),
            dma((chunks, n_all)),
            dma((chunks, n_all)),
        ],
        compiler_params=pltpu.CompilerParams(
            collective_id=0, has_side_effects=True, vmem_limit_bytes=60 * 1024 * 1024
        ),
        name="core",
    )(query, key, value, cotangent, weights, *consts)
    flat = jax.ShapeDtypeStruct((rows, width), BF16)
    outs = pl.pallas_call(
        after_kernel,
        out_shape=[flat, flat, flat, flat, jax.ShapeDtypeStruct((tap_rows * n_chan, width), F32)],
        in_specs=whole_vmem(7),
        out_specs=whole_vmem(5),
        scratch_shapes=[pltpu.VMEM((width, fast), F32)],
        compiler_params=pltpu.CompilerParams(vmem_limit_bytes=24 * 1024 * 1024),
        name="after",
    )(query, key, value, cotangent, skip_gain.reshape(1, width), sig, taps)
    return (*outs[:4], outs[4].reshape(tap_rows, 1, all_width))


def solution(mesh):
    n_chan, n_seq = mesh.shape["chan"], mesh.shape["seq"]
    block = P("seq", "chan")
    taps = P("chan", "seq", None)
    return jax.shard_map(
        functools.partial(body, n_chan, n_seq),
        mesh=mesh,
        in_specs=(block, block, block, taps, P("chan"), block),
        out_specs=(block, block, block, block, taps),
        check_vma=False,
    )
```
